128 devices in a mesh: rows: 16 (over z, x), cols: 8 (over y, core).
Axes of the slice: x: 4, y: 4, z: 4, core: 2. Of those that a mesh axis runs over, the one named last changes fastest.
Arguments:
- trailing: bfloat16 [32, 16, 1024, 1024], P('rows', 'cols'), may hold values from -6 to 6
- row_left: bfloat16 [3, 32, 1024, 384], P(None, 'rows', 'cols'), may hold values from -0.5 to 0.5
- row_right: bfloat16 [3, 32, 1024, 384], P(None, 'rows', 'cols'), may hold values from -0.5 to 0.5
- column_left: bfloat16 [3, 16, 1024, 384], P(None, 'cols', 'rows'), may hold values from -0.5 to 0.5
- column_right: bfloat16 [3, 16, 1024, 384], P(None, 'cols', 'rows'), may hold values from -0.5 to 0.5
- row_ranks: int32 [3, 32], replicated, may hold values from 64 to 384, as said below
- column_ranks: int32 [3, 16], P(None, 'cols'), may hold values from 64 to 384, as said below
Outputs:
- updated: float32 [32, 16, 1024, 1024], P('rows', 'cols')
The draws below stay inside these ranges and needn't reach their ends.
Inputs may be any that keep to these rules, and one draw needn't show every extreme that they name: `row_ranks`: every rank is a multiple of 64. `column_ranks`: every rank is a multiple of 64.
All inputs are finite; a program needn't handle non-finite values.
Results may differ from the reference program's by a relative error of at most 0.0026.
Values may be sent and summed in bfloat16 or wider, within the bound.
A program may use at most 128 MiB of HBM per device.

```python
import jax
import jax.numpy as jnp
from jax import lax

B = 1024
RB = 64
R = 384
K = 3
TROWS = 32
TCOLS = 16


def draw_row_ranks(key, part):
    positions = jnp.arange(TROWS, dtype=jnp.int32)
    quarter = 4 * positions // TROWS
    base = jnp.where(quarter == 0, 5, jnp.where(quarter == 1, 2, 1)).astype(jnp.int32)
    extra = jax.random.randint(jax.random.fold_in(key, 11), (K, TROWS), 0, 2).astype(jnp.int32)
    blocks = jnp.clip(base[None, :] + extra, 1, 6)
    blocks = blocks.at[0, 0].set(6).at[K - 1, TROWS - 1].set(1)
    return (blocks * RB).astype(jnp.int32)


def draw_column_ranks(key, part):
    blocks = jax.random.randint(jax.random.fold_in(key, 23), (K, TCOLS), 1, 7).astype(jnp.int32)
    blocks = blocks.at[0, 0].set(6).at[K - 1, TCOLS - 1].set(1)
    return (blocks * RB).astype(jnp.int32)


def block_scale(rng, dims, shards, least, high):
    factor_of, own = 1.0, jax.random.fold_in(rng, 6)
    for position, blocks in shards:
        steps = jnp.exp(jax.random.uniform(jax.random.fold_in(own, position), (blocks,), jnp.float32, least / len(shards), high / len(shards)))
        factor_of = factor_of * jnp.repeat(steps, dims[position] // blocks).reshape([-1 if axis == position else 1 for axis in range(len(dims))])
    return factor_of


def noise(stream_key, extent, scale, bound, split=(), held_as=jnp.bfloat16):
    entries = jax.random.normal(stream_key, extent, jnp.float32) * scale
    if len(split) > 0:
        entries = block_scale(stream_key, extent, split, -0.22, 0.18) * entries
    return jnp.clip(entries, min=-bound, max=bound).astype(held_as)


def setup_inputs(seed: int = 0) -> dict:
    arg_keys = jax.random.split(jax.random.key(seed), 8)
    trailing = noise(arg_keys[0], (TROWS, TCOLS, B, B), 1.0, 6.0, ((0, 16), (1, 8)))
    row_left = noise(arg_keys[1], (K, TROWS, B, R), ((B * R * R) ** 0.25) ** -0.5, 0.5, ((1, 16), (2, 8)))
    row_right = noise(arg_keys[2], (K, TROWS, B, R), ((B * R * R) ** 0.25) ** -0.5, 0.5, ((1, 16), (2, 8)))
    column_left = noise(arg_keys[3], (K, TCOLS, B, R), ((B * R * R) ** 0.25) ** -0.5, 0.5, ((1, 8), (2, 16)))
    column_right = noise(arg_keys[4], (K, TCOLS, B, R), ((B * R * R) ** 0.25) ** -0.5, 0.5, ((1, 8), (2, 16)))
    row_ranks = draw_row_ranks(jax.random.fold_in(arg_keys[7], 71), 0)
    column_ranks = draw_column_ranks(jax.random.fold_in(arg_keys[7], 71), 0)
    return {"trailing": trailing, "row_left": row_left, "row_right": row_right, "column_left": column_left, "column_right": column_right, "row_ranks": row_ranks, "column_ranks": column_ranks}


def reference(trailing, row_left, row_right, column_left, column_right, row_ranks, column_ranks):
    width = row_left.shape[3]
    keep_mask = (jnp.arange(width, dtype=jnp.int32)[None, None, :] < column_ranks[:, :, None]).astype(column_left.dtype)
    masked_left = column_left * keep_mask[:, :, None, :]
    masked_right = column_right * keep_mask[:, :, None, :]

    def one_row(row_index):
        totals = jnp.zeros((trailing.shape[1], trailing.shape[2], trailing.shape[3]), jnp.float32)
        for panel in range(K):
            left_tile = row_left[panel, row_index]
            right_tile = row_right[panel, row_index]
            cols_left = masked_left[panel].astype(jnp.float32)
            cols_right = masked_right[panel].astype(jnp.float32)
            blocks_used = row_ranks[panel, row_index] // RB

            def one_block(turn, carry):
                start = (turn * RB).astype(jnp.int32)
                left_block = lax.dynamic_slice_in_dim(left_tile, start, RB, 1).astype(jnp.float32)
                right_block = lax.dynamic_slice_in_dim(right_tile, start, RB, 1).astype(jnp.float32)
                core_block = jnp.einsum("bk,jbr->jkr", right_block, cols_right).astype(jnp.bfloat16)
                projected = jnp.einsum("jkr,jcr->jkc", core_block.astype(jnp.float32), cols_left).astype(jnp.bfloat16)
                return carry + jnp.einsum("bk,jkc->jbc", left_block, projected.astype(jnp.float32))

            totals = lax.fori_loop(jnp.int32(0), blocks_used.astype(jnp.int32), one_block, totals)
        return trailing[row_index].astype(jnp.float32) - totals

    return lax.map(one_row, jnp.arange(trailing.shape[0], dtype=jnp.int32))
```

```python
import jax
import jax.numpy as jnp
from jax import lax
from jax.experimental import pallas as pl
from jax.experimental.pallas import tpu as pltpu
from jax.sharding import PartitionSpec as P

SIDE = 4
MESH = pl.DeviceIdType.MESH


class Grid:
    def __init__(self):
        self.r = lax.axis_index("rows")
        self.c = lax.axis_index("cols")
        self.z, self.x = self.r // SIDE, self.r % SIDE
        self.y, self.core = self.c // 2, self.c % 2

    def shifted(self, axis, step):
        return (getattr(self, axis) + (step + SIDE)) % SIDE

    def neighbour(self, axis, step):
        if axis == "z":
            return (self.shifted("z", step) * SIDE + self.x, self.c)
        if axis == "x":
            return (self.z * SIDE + self.shifted("x", step), self.c)
        if axis == "y":
            return (self.r, self.shifted("y", step) * 2 + self.core)
        return (self.r, self.y * 2 + (1 - self.core))


class Messages:
    def __init__(self, send_sem, recv_sem):
        self.send_sem, self.recv_sem = send_sem, recv_sem
        self.sent = {}

    def send(self, key, view, target):
        index = len(self.sent)
        copy = pltpu.make_async_remote_copy(
            src_ref=view,
            dst_ref=view,
            send_sem=self.send_sem.at[index],
            recv_sem=self.recv_sem.at[index],
            device_id=target,
            device_id_type=MESH,
        )
        copy.start()
        self.sent[key] = copy

    def got(self, key):
        self.sent[key].wait_recv()

    def drain(self):
        for copy in self.sent.values():
            copy.wait_send()


class ColumnStream:
    def __init__(self, name, grid, messages, buf, first, second):
        self.name, self.grid, self.messages, self.buf = name, grid, messages, buf
        self.a, self.b = first, second

    def view(self, da, db, half=None):
        place = {self.a: self.grid.shifted(self.a, da), self.b: self.grid.shifted(self.b, db)}
        if half is None:
            return self.buf.at[:, place["z"], place["x"]]
        part = self.buf.shape[3] // 2
        return self.buf.at[:, place["z"], place["x"], pl.ds(half * part, part)]

    def send(self, kind, da, db, axis, step, half=None):
        self.messages.send(
            (self.name, kind, da, step), self.view(da, db, half), self.grid.neighbour(axis, step)
        )

    def got(self, kind, da, step):
        self.messages.got((self.name, kind, da, step))

    def start_a(self):
        for step in (1, -1):
            self.send("a", 0, 0, self.a, step)

    def start_b(self):
        for step in (1, -1):
            self.send("b", 0, 0, self.b, step)

    def e1(self):
        for step in (1, -1):
            self.got("a", 0, step)
            self.messages.send(
                (self.name, "ah", 0, step),
                self.view(-step, 0, 0 if step == 1 else 1),
                self.grid.neighbour(self.a, step),
            )
            for out in (1, -1):
                self.send("b", -step, 0, self.b, out)

    def relay(self, da):
        for step in (1, -1):
            self.got("b", da, step)
            self.send("bh", da, -step, self.b, step, 0 if step == 1 else 1)

    def e2(self):
        self.relay(0)

    def e3(self):
        for step in (1, -1):
            self.got("ah", 0, step)
        for out in (1, -1):
            self.send("b", 2, 0, self.b, out)

    def e4(self):
        self.relay(1)
        self.relay(-1)

    def e5(self):
        self.relay(2)

    def e6(self):
        for da in (0, 1, -1, 2):
            for step in (1, -1):
                self.got("bh", da, step)


class RowStream:
    def __init__(self, name, grid, messages, buf):
        self.name, self.grid, self.messages, self.buf = name, grid, messages, buf

    def view(self, dy, half=None):
        place = self.grid.shifted("y", dy) * 2 + self.grid.core
        if half is None:
            return self.buf.at[:, place]
        part = self.buf.shape[2] // 2
        return self.buf.at[:, place, pl.ds(half * part, part)]

    def share(self, dy):
        self.messages.send((self.name, "s", dy), self.view(dy), self.grid.neighbour("core", 1))

    def start(self):
        for step in (1, -1):
            self.messages.send(
                (self.name, "y", step), self.view(0), self.grid.neighbour("y", step)
            )
        self.share(0)

    def e1(self):
        for step in (1, -1):
            self.messages.got((self.name, "y", step))
            self.messages.send(
                (self.name, "yh", step),
                self.view(-step, 0 if step == 1 else 1),
                self.grid.neighbour("y", step),
            )
            self.share(-step)

    def e3(self):
        for step in (1, -1):
            self.messages.got((self.name, "yh", step))
        self.share(2)

    def e6(self):
        for dy in (0, 1, -1, 2):
            self.messages.got((self.name, "s", dy))


MESSAGES = 4 * 20 + 4 * 8


def gather_kernel(
    row_ranks, column_ranks, row_left, row_right, column_left, column_right,
    left_out, right_out,
    col_v, col_u, row_v, row_u, core, right, send_sem, recv_sem, local_sem, out_sem,
):
    grid = Grid()
    panels = row_left.shape[0]
    loads = []
    for tile in range(2):
        for source, target in ((column_right, col_v), (column_left, col_u)):
            loads.append((source.at[:, tile], target.at[tile, :, grid.z, grid.x]))
        for source, target in ((row_right, row_v), (row_left, row_u)):
            loads.append((source.at[:, tile], target.at[tile, :, grid.c]))
    loads = [
        pltpu.make_async_copy(source, target, local_sem.at[n])
        for n, (source, target) in enumerate(loads)
    ]
    for load in loads:
        load.start()
    barrier = pltpu.get_barrier_semaphore()
    for axis, step in (("x", 1), ("x", -1), ("z", 1), ("z", -1), ("y", 1), ("y", -1), ("core", 1)):
        pl.semaphore_signal(
            barrier, inc=1, device_id=grid.neighbour(axis, step), device_id_type=MESH
        )
    pl.semaphore_wait(barrier, 7)
    for load in loads:
        load.wait()

    messages = Messages(send_sem, recv_sem)
    v = [
        ColumnStream("v0", grid, messages, col_v.at[0], "x", "z"),
        ColumnStream("v1", grid, messages, col_v.at[1], "z", "x"),
    ]
    u = [
        ColumnStream("u0", grid, messages, col_u.at[0], "x", "z"),
        ColumnStream("u1", grid, messages, col_u.at[1], "z", "x"),
    ]
    rv = [RowStream(f"rv{tile}", grid, messages, row_v.at[tile]) for tile in range(2)]
    ru = [RowStream(f"ru{tile}", grid, messages, row_u.at[tile]) for tile in range(2)]

    def all_of(streams, *names):
        for name in names:
            for stream in streams:
                getattr(stream, name)()

    def cores(col, row):
        rank_c = lax.broadcasted_iota(jnp.int32, core.shape[3:], 0)
        rank_r = lax.broadcasted_iota(jnp.int32, core.shape[3:], 1)

        def one(panel, carry):
            rows, width = SIDE * SIDE * col_v.shape[4], col_v.shape[5]
            value = lax.dot_general(
                col_v[col, panel].reshape(rows, width),
                row_v[row, panel].reshape(rows, width),
                (((0,), (0,)), ((), ())),
                preferred_element_type=jnp.float32,
            )
            keep = (rank_c < column_ranks[panel, col]) & (
                rank_r < row_ranks[panel, grid.r * 2 + row]
            )
            core[col, row, panel] = jnp.where(keep, value, 0.0).astype(core.dtype)
            return carry

        lax.fori_loop(0, panels, one, 0)

    stores = []

    def rights(col, step):
        depth, width = SIDE * col_u.shape[4], col_u.shape[5]
        place = grid.shifted("z" if col == 0 else "x", step)

        def one(turn, carry):
            panel, row = turn // 2, turn % 2
            if col == 0:
                factor = col_u[0, panel, place]
            else:
                factor = col_u[1, panel, :, place]
            value = jnp.dot(
                factor.reshape(depth, width),
                core[col, row, panel],
                preferred_element_type=jnp.float32,
            )
            value = value.astype(right.dtype).reshape(factor.shape)
            if col == 0:
                right[row, 0, panel, place] = value
            else:
                right[row, 1, panel, :, place] = value
            return carry

        lax.fori_loop(0, 2 * panels, one, 0)
        if col == 0:
            source, target = right.at[:, 0, :, place], right_out.at[:, 0, :, place]
        else:
            source, target = right.at[:, 1, :, :, place], right_out.at[:, 1, :, :, place]
        store = pltpu.make_async_copy(source, target, out_sem.at[len(stores)])
        store.start()
        stores.append(store)

    all_of(v, "start_a", "start_b")
    all_of(rv, "start")
    all_of(v, "e1")
    all_of(rv, "e1")
    all_of(v, "e2", "e3")
    all_of(u, "start_a", "start_b")
    all_of(rv, "e3")
    all_of(ru, "start")
    all_of(v, "e4", "e5")
    all_of(u, "e1")
    all_of(ru, "e1")
    all_of(v, "e6")
    all_of(u, "e2")
    all_of(rv, "e6")
    cores(0, 0)
    all_of(u, "e3")
    all_of(ru, "e3")
    cores(0, 1)
    all_of(u, "e4")
    cores(1, 0)
    all_of(u, "e5")
    cores(1, 1)
    all_of(ru, "e6")
    store = pltpu.make_async_copy(row_u, left_out, out_sem.at[0])
    store.start()
    stores.append(store)
    for step in (0, 1, -1):
        for col in range(2):
            rights(col, step)
    for col in range(2):
        u[col].e6()
        rights(col, 2)
    messages.drain()
    for store in stores:
        store.wait()


def gather(row_ranks, column_ranks, row_left, row_right, column_left, column_right):
    panels, rows_here, depth_r, width = row_left.shape
    depth_c = column_left.shape[2]
    bf16 = jnp.bfloat16
    any_space = pl.BlockSpec(memory_space=pl.ANY)
    smem = pl.BlockSpec(memory_space=pltpu.SMEM)
    left_shape = (rows_here, panels, 8, depth_r, width)
    col_shape = (2, panels, SIDE, SIDE, depth_c, width)
    right_shape = (rows_here, 2, panels, SIDE, SIDE, depth_c, width)
    return pl.pallas_call(
        gather_kernel,
        out_shape=(
            jax.ShapeDtypeStruct(left_shape, bf16),
            jax.ShapeDtypeStruct(right_shape, bf16),
        ),
        in_specs=[smem, smem] + [any_space] * 4,
        out_specs=(any_space, any_space),
        scratch_shapes=[
            pltpu.VMEM(col_shape, bf16),
            pltpu.VMEM(col_shape, bf16),
            pltpu.VMEM(left_shape, bf16),
            pltpu.VMEM(left_shape, bf16),
            pltpu.VMEM((2, rows_here, panels, width, width), bf16),
            pltpu.VMEM(right_shape, bf16),
            pltpu.SemaphoreType.DMA((MESSAGES,)),
            pltpu.SemaphoreType.DMA((MESSAGES,)),
            pltpu.SemaphoreType.DMA((8,)),
            pltpu.SemaphoreType.DMA((9,)),
        ],
        compiler_params=pltpu.CompilerParams(
            collective_id=0, has_side_effects=True, vmem_limit_bytes=60 << 20
        ),
        name="gather",
    )(row_ranks, column_ranks, row_left, row_right, column_left, column_right)


def update_kernel(trailing, left, right, out):
    total = trailing[0, 0].astype(jnp.float32)
    for panel in range(left.shape[1]):
        total = total - lax.dot_general(
            left[0, panel],
            right[0, 0, panel],
            (((1,), (1,)), ((), ())),
            preferred_element_type=jnp.float32,
        )
    out[0, 0] = total


def subtract(trailing, left, right):
    rows_here, cols_here, order, _ = trailing.shape
    panels, width = left.shape[1], left.shape[3]
    block = 256
    return pl.pallas_call(
        update_kernel,
        out_shape=jax.ShapeDtypeStruct(trailing.shape, jnp.float32),
        grid=(rows_here, cols_here, order // block),
        in_specs=[
            pl.BlockSpec((1, 1, block, order), lambda i, j, b: (i, j, b, 0)),
            pl.BlockSpec((1, panels, block, width), lambda i, j, b: (i, 0, b, 0)),
            pl.BlockSpec((1, 1, panels, order, width), lambda i, j, b: (i, j, 0, 0, 0)),
        ],
        out_specs=pl.BlockSpec((1, 1, block, order), lambda i, j, b: (i, j, b, 0)),
        compiler_params=pltpu.CompilerParams(vmem_limit_bytes=48 << 20),
        name="subtract",
    )(trailing, left, right)


def on_device(trailing, row_left, row_right, column_left, column_right, row_ranks, column_ranks):
    left, right = gather(row_ranks, column_ranks, row_left, row_right, column_left, column_right)
    rows_here, cols_here, order, _ = trailing.shape
    panels, width = row_left.shape[0], row_left.shape[3]
    left = left.reshape(rows_here, panels, order, width)
    right = right.reshape(rows_here, cols_here, panels, order, width)
    return subtract(trailing, left, right)


def solution(mesh):
    return jax.shard_map(
        on_device,
        mesh=mesh,
        in_specs=(
            P("rows", "cols", None, None),
            P(None, "rows", "cols", None),
            P(None, "rows", "cols", None),
            P(None, "cols", "rows", None),
            P(None, "cols", "rows", None),
            P(),
            P(None, "cols"),
        ),
        out_specs=P("rows", "cols", None, None),
        check_vma=False,
    )
```

```python
import jax
import jax.numpy as jnp
from jax import lax
from jax.experimental import pallas as pl
from jax.experimental.pallas import tpu as pltpu
from jax.sharding import PartitionSpec as P

SIDE = 4
MESH = pl.DeviceIdType.MESH


class Grid:
    def __init__(self):
        self.r = lax.axis_index("rows")
        self.c = lax.axis_index("cols")
        self.z, self.x = self.r // SIDE, self.r % SIDE
        self.y, self.core = self.c // 2, self.c % 2

    def shifted(self, axis, step):
        return (getattr(self, axis) + (step + SIDE)) % SIDE

    def neighbour(self, axis, step):
        if axis == "z":
            return (self.shifted("z", step) * SIDE + self.x, self.c)
        if axis == "x":
            return (self.z * SIDE + self.shifted("x", step), self.c)
        if axis == "y":
            return (self.r, self.shifted("y", step) * 2 + self.core)
        return (self.r, self.y * 2 + (1 - self.core))


class Messages:
    def __init__(self, send_sem, recv_sem):
        self.send_sem, self.recv_sem = send_sem, recv_sem
        self.sent = {}

    def send(self, key, view, target):
        index = len(self.sent)
        copy = pltpu.make_async_remote_copy(
            src_ref=view,
            dst_ref=view,
            send_sem=self.send_sem.at[index],
            recv_sem=self.recv_sem.at[index],
            device_id=target,
            device_id_type=MESH,
        )
        copy.start()
        self.sent[key] = copy

    def got(self, key):
        self.sent[key].wait_recv()

    def drain(self):
        for copy in self.sent.values():
            copy.wait_send()


class ColumnStream:
    def __init__(self, name, grid, messages, buf, first, second):
        self.name, self.grid, self.messages, self.buf = name, grid, messages, buf
        self.a, self.b = first, second

    def view(self, da, db, half=None):
        place = {self.a: self.grid.shifted(self.a, da), self.b: self.grid.shifted(self.b, db)}
        if half is None:
            return self.buf.at[:, place["z"], place["x"]]
        part = self.buf.shape[3] // 2
        return self.buf.at[:, place["z"], place["x"], pl.ds(half * part, part)]

    def send(self, kind, da, db, axis, step, half=None):
        self.messages.send(
            (self.name, kind, da, step), self.view(da, db, half), self.grid.neighbour(axis, step)
        )

    def got(self, kind, da, step):
        self.messages.got((self.name, kind, da, step))

    def start_a(self):
        for step in (1, -1):
            self.send("a", 0, 0, self.a, step)

    def start_b(self):
        for step in (1, -1):
            self.send("b", 0, 0, self.b, step)

    def e1(self):
        for step in (1, -1):
            self.got("a", 0, step)
            self.messages.send(
                (self.name, "ah", 0, step),
                self.view(-step, 0, 0 if step == 1 else 1),
                self.grid.neighbour(self.a, step),
            )
            for out in (1, -1):
                self.send("b", -step, 0, self.b, out)

    def relay(self, da):
        for step in (1, -1):
            self.got("b", da, step)
            self.send("bh", da, -step, self.b, step, 0 if step == 1 else 1)

    def e2(self):
        self.relay(0)

    def e3(self):
        for step in (1, -1):
            self.got("ah", 0, step)
        for out in (1, -1):
            self.send("b", 2, 0, self.b, out)

    def e4(self):
        self.relay(1)
        self.relay(-1)

    def e5(self):
        self.relay(2)

    def e6(self):
        for da in (0, 1, -1, 2):
            for step in (1, -1):
                self.got("bh", da, step)


class RowStream:
    def __init__(self, name, grid, messages, buf):
        self.name, self.grid, self.messages, self.buf = name, grid, messages, buf

    def view(self, dy, half=None):
        place = self.grid.shifted("y", dy)
        if half is None:
            return self.buf.at[:, place, self.grid.core]
        part = self.buf.shape[3] // 2
        return self.buf.at[:, place, self.grid.core, pl.ds(half * part, part)]

    def share(self, dy):
        self.messages.send((self.name, "s", dy), self.view(dy), self.grid.neighbour("core", 1))

    def start(self):
        for step in (1, -1):
            self.messages.send(
                (self.name, "y", step), self.view(0), self.grid.neighbour("y", step)
            )
        self.share(0)

    def e1(self):
        for step in (1, -1):
            self.messages.got((self.name, "y", step))
            self.messages.send(
                (self.name, "yh", step),
                self.view(-step, 0 if step == 1 else 1),
                self.grid.neighbour("y", step),
            )
            self.share(-step)

    def e3(self):
        for step in (1, -1):
            self.messages.got((self.name, "yh", step))
        self.share(2)

    def e6(self):
        for dy in (0, 1, -1, 2):
            self.messages.got((self.name, "s", dy))


MESSAGES = 4 * 20 + 2 * 8


def gather_kernel(
    row_ranks, column_ranks, trailing, row_left, row_right, column_left, column_right,
    out,
    col_v, col_u, row_v, row_u, total, core, right, dense, send_sem, recv_sem, local_sem,
):
    grid = Grid()
    panels, tiles, depth_r, width = row_left.shape
    depth_c = column_left.shape[2]
    chunk = SIDE * depth_c
    loads = []
    for tile in range(2):
        for source, target in ((column_right, col_v), (column_left, col_u)):
            loads.append((source.at[:, tile], target.at[tile, :, grid.z, grid.x]))
        lanes = pl.ds(tile * width, width)
        loads.append((row_right.at[:, tile], row_v.at[:, grid.y, grid.core, :, lanes]))
    for panel in range(panels):
        lanes = pl.ds(panel * width, width)
        loads.append((row_left.at[panel], row_u.at[:, grid.y, grid.core, :, lanes]))
    loads.append((trailing, dense))
    loads = [
        pltpu.make_async_copy(source, target, local_sem.at[n])
        for n, (source, target) in enumerate(loads)
    ]
    for load in loads:
        load.start()
    barrier = pltpu.get_barrier_semaphore()
    for axis, step in (("x", 1), ("x", -1), ("z", 1), ("z", -1), ("y", 1), ("y", -1), ("core", 1)):
        pl.semaphore_signal(
            barrier, inc=1, device_id=grid.neighbour(axis, step), device_id_type=MESH
        )
    pl.semaphore_wait(barrier, 7)
    for load in loads[:-1]:
        load.wait()

    messages = Messages(send_sem, recv_sem)
    v = [
        ColumnStream("v0", grid, messages, col_v.at[0], "x", "z"),
        ColumnStream("v1", grid, messages, col_v.at[1], "z", "x"),
    ]
    u = [
        ColumnStream("u0", grid, messages, col_u.at[0], "x", "z"),
        ColumnStream("u1", grid, messages, col_u.at[1], "z", "x"),
    ]
    rv = [RowStream("rv", grid, messages, row_v)]
    ru = [RowStream("ru", grid, messages, row_u)]

    def all_of(streams, *names):
        for name in names:
            for stream in streams:
                getattr(stream, name)()

    def widen():
        def one(turn, carry):
            rows = pl.ds(pl.multiple_of((turn % 4) * chunk, chunk), chunk)
            out[turn // 4, 1, rows] = dense[turn // 4, 1, rows].astype(jnp.float32)
            return carry

        lax.fori_loop(0, 4 * tiles, one, 0)

    def cores(col, step, first=False, last=False):
        place = grid.shifted("z" if col == 0 else "x", step)

        def one(panel, carry):
            if col == 0:
                left_side, right_side = col_v[0, panel, place], row_v[panel, place]
            else:
                start = pl.multiple_of((place % 2) * depth_c, depth_c)
                left_side = col_v[1, panel, :, place]
                right_side = row_v[panel, :, place // 2, pl.ds(start, depth_c)]
            value = lax.dot_general(
                left_side.reshape(chunk, width),
                right_side.reshape(chunk, tiles * width),
                (((0,), (0,)), ((), ())),
                preferred_element_type=jnp.float32,
            )
            if not first:
                value = value + total[col, panel]
            if last:
                shape = value.shape
                lane = lax.broadcasted_iota(jnp.int32, shape, 1)
                limit = jnp.where(
                    lane < width,
                    row_ranks[panel, grid.r * 2],
                    row_ranks[panel, grid.r * 2 + 1] + width,
                )
                keep = (lane < limit) & (
                    lax.broadcasted_iota(jnp.int32, shape, 0) < column_ranks[col, panel]
                )
                core[col, panel] = jnp.where(keep, value, 0.0).astype(core.dtype)
            else:
                total[col, panel] = value
            return carry

        lax.fori_loop(0, panels, one, 0)

    def updates(col, step):
        place = grid.shifted("z" if col == 0 else "x", step)
        half = place % 2
        for panel in range(panels):
            factor = col_u[0, panel, place] if col == 0 else col_u[1, panel, :, place]
            value = jnp.dot(
                factor.reshape(chunk, width), core[col, panel], preferred_element_type=jnp.float32
            ).astype(right.dtype)
            for tile in range(tiles):
                lanes = pl.ds(panel * width, width)
                piece = value[:, tile * width : (tile + 1) * width]
                if col == 0:
                    right[tile, :, lanes] = piece
                    continue
                for group in range(SIDE):
                    side = half if group < 2 else 1 - half
                    start = pl.multiple_of((group % 2) * 2 * depth_c + side * depth_c, depth_c)
                    right[tile, pl.ds(start, depth_c), lanes] = piece[
                        group * depth_c : (group + 1) * depth_c
                    ]

        def one(turn, carry):
            tile, part = turn // 2, turn % 2
            rows = 2 * chunk
            value = lax.dot_general(
                row_u[tile, pl.ds(part * 2, 2)].reshape(rows, panels * width),
                right[tile],
                (((1,), (1,)), ((), ())),
                preferred_element_type=jnp.float32,
            )
            here = pl.ds(pl.multiple_of(part * rows, rows), rows)
            if col == 0:
                lanes = pl.ds(pl.multiple_of(place * chunk, chunk), chunk)
                out[tile, 0, here, lanes] = dense[tile, 0, here, lanes].astype(jnp.float32) - value
                return carry
            span = 2 * depth_c
            mine = lax.broadcasted_iota(jnp.int32, (rows, span), 1) // depth_c == half
            for group in range(SIDE):
                piece = value[:, (group % 2) * span : (group % 2 + 1) * span]
                if group >= 2:
                    piece = pltpu.roll(piece, depth_c, 1)
                lanes = pl.ds(pl.multiple_of((group * 2 + place // 2) * span, span), span)
                out[tile, 1, here, lanes] = out[tile, 1, here, lanes] - jnp.where(mine, piece, 0.0)
            return carry

        lax.fori_loop(0, 2 * tiles, one, 0)

    all_of(v, "start_a", "start_b")
    all_of(rv, "start")
    all_of(v, "e1")
    loads[-1].wait()
    widen()
    all_of(v, "e2")
    all_of(rv, "e1")
    all_of(v, "e3")
    all_of(u, "start_a", "start_b")
    all_of(rv, "e3")
    all_of(ru, "start")
    all_of(v, "e4", "e5")
    all_of(u, "e1")
    all_of(rv, "e6")
    for col in range(2):
        cores(col, 0, first=True)
    all_of(u, "e2")
    for col in range(2):
        cores(col, 1)
    all_of(ru, "e1")
    for col in range(2):
        cores(col, -1)
    all_of(u, "e3")
    all_of(v, "e6")
    for col in range(2):
        cores(col, 2, last=True)
    all_of(u, "e4")
    all_of(ru, "e3", "e6")
    updates(0, 0)
    all_of(u, "e5")
    updates(1, 0)
    for step in (1, -1):
        for col in range(2):
            updates(col, step)
    for col in range(2):
        u[col].e6()
        updates(col, 2)
    messages.drain()


def on_device(trailing, row_left, row_right, column_left, column_right, row_ranks, column_ranks):
    panels, tiles, depth_r, width = row_left.shape
    depth_c = column_left.shape[2]
    order = trailing.shape[3]
    bf16 = jnp.bfloat16
    any_space = pl.BlockSpec(memory_space=pl.ANY)
    smem = pl.BlockSpec(memory_space=pltpu.SMEM)
    col_shape = (2, panels, SIDE, SIDE, depth_c, width)
    return pl.pallas_call(
        gather_kernel,
        out_shape=pltpu.VMEM(trailing.shape, jnp.float32),
        in_specs=[smem, smem] + [any_space] * 5,
        out_specs=pl.BlockSpec(memory_space=pltpu.VMEM),
        scratch_shapes=[
            pltpu.VMEM(col_shape, bf16),
            pltpu.VMEM(col_shape, bf16),
            pltpu.VMEM((panels, SIDE, 2, depth_r, tiles * width), bf16),
            pltpu.VMEM((tiles, SIDE, 2, depth_r, panels * width), bf16),
            pltpu.VMEM((2, panels, width, tiles * width), jnp.float32),
            pltpu.VMEM((2, panels, width, tiles * width), bf16),
            pltpu.VMEM((tiles, SIDE * depth_c, panels * width), bf16),
            pltpu.VMEM(trailing.shape, bf16),
            pltpu.SemaphoreType.DMA((MESSAGES,)),
            pltpu.SemaphoreType.DMA((MESSAGES,)),
            pltpu.SemaphoreType.DMA((10,)),
        ],
        compiler_params=pltpu.CompilerParams(
            collective_id=0, has_side_effects=True, vmem_limit_bytes=LIMIT
        ),
        name="gather_update",
    )(row_ranks, column_ranks.T, trailing, row_left, row_right, column_left, column_right)


LIMIT = 46 << 20


def solution(mesh):
    return jax.shard_map(
        on_device,
        mesh=mesh,
        in_specs=(
            P("rows", "cols", None, None),
            P(None, "rows", "cols", None),
            P(None, "rows", "cols", None),
            P(None, "cols", "rows", None),
            P(None, "cols", "rows", None),
            P(),
            P(None, "cols"),
        ),
        out_specs=P("rows", "cols", None, None),
        check_vma=False,
    )
```

```python
import jax
import jax.numpy as jnp
from jax import lax
from jax.experimental import pallas as pl
from jax.experimental.pallas import tpu as pltpu
from jax.sharding import PartitionSpec as P

SIDE = 4
MESH = pl.DeviceIdType.MESH


class Grid:
    def __init__(self):
        self.r = lax.axis_index("rows")
        self.c = lax.axis_index("cols")
        self.z, self.x = self.r // SIDE, self.r % SIDE
        self.y, self.core = self.c // 2, self.c % 2

    def shifted(self, axis, step):
        return (getattr(self, axis) + (step + SIDE)) % SIDE

    def neighbour(self, axis, step):
        if axis == "z":
            return (self.shifted("z", step) * SIDE + self.x, self.c)
        if axis == "x":
            return (self.z * SIDE + self.shifted("x", step), self.c)
        if axis == "y":
            return (self.r, self.shifted("y", step) * 2 + self.core)
        return (self.r, self.y * 2 + (1 - self.core))


class Messages:
    def __init__(self, send_sem, recv_sem):
        self.send_sem, self.recv_sem = send_sem, recv_sem
        self.sent = {}

    def send(self, key, view, target):
        index = len(self.sent)
        copy = pltpu.make_async_remote_copy(
            src_ref=view,
            dst_ref=view,
            send_sem=self.send_sem.at[index],
            recv_sem=self.recv_sem.at[index],
            device_id=target,
            device_id_type=MESH,
        )
        copy.start()
        self.sent[key] = copy

    def got(self, key):
        self.sent[key].wait_recv()

    def drain(self):
        for copy in self.sent.values():
            copy.wait_send()


class ColumnStream:
    def __init__(self, name, grid, messages, buf, first, second):
        self.name, self.grid, self.messages, self.buf = name, grid, messages, buf
        self.a, self.b = first, second

    def view(self, da, db, half=None):
        place = {self.a: self.grid.shifted(self.a, da), self.b: self.grid.shifted(self.b, db)}
        if half is None:
            return self.buf.at[:, place["z"], place["x"]]
        part = self.buf.shape[3] // 2
        return self.buf.at[:, place["z"], place["x"], pl.ds(half * part, part)]

    def send(self, kind, da, db, axis, step, half=None):
        self.messages.send(
            (self.name, kind, da, step), self.view(da, db, half), self.grid.neighbour(axis, step)
        )

    def got(self, kind, da, step):
        self.messages.got((self.name, kind, da, step))

    def start_a(self):
        for step in (1, -1):
            self.send("a", 0, 0, self.a, step)

    def start_b(self):
        for step in (1, -1):
            self.send("b", 0, 0, self.b, step)

    def e1(self):
        for step in (1, -1):
            self.got("a", 0, step)
            self.messages.send(
                (self.name, "ah", 0, step),
                self.view(-step, 0, 0 if step == 1 else 1),
                self.grid.neighbour(self.a, step),
            )
            for out in (1, -1):
                self.send("b", -step, 0, self.b, out)

    def relay(self, da):
        for step in (1, -1):
            self.got("b", da, step)
            self.send("bh", da, -step, self.b, step, 0 if step == 1 else 1)

    def e2(self):
        self.relay(0)

    def e3(self):
        for step in (1, -1):
            self.got("ah", 0, step)
        for out in (1, -1):
            self.send("b", 2, 0, self.b, out)

    def e4(self):
        self.relay(1)
        self.relay(-1)

    def e5(self):
        self.relay(2)

    def e6(self):
        for da in (0, 1, -1, 2):
            for step in (1, -1):
                self.got("bh", da, step)


class RowStream:
    def __init__(self, name, grid, messages, buf):
        self.name, self.grid, self.messages, self.buf = name, grid, messages, buf

    def view(self, dy, half=None):
        place = self.grid.shifted("y", dy)
        if half is None:
            return self.buf.at[:, place, self.grid.core]
        part = self.buf.shape[3] // 2
        return self.buf.at[:, place, self.grid.core, pl.ds(half * part, part)]

    def share(self, dy):
        self.messages.send((self.name, "s", dy), self.view(dy), self.grid.neighbour("core", 1))

    def start(self):
        for step in (1, -1):
            self.messages.send(
                (self.name, "y", step), self.view(0), self.grid.neighbour("y", step)
            )
        self.share(0)

    def e1(self):
        for step in (1, -1):
            self.messages.got((self.name, "y", step))
            self.messages.send(
                (self.name, "yh", step),
                self.view(-step, 0 if step == 1 else 1),
                self.grid.neighbour("y", step),
            )
            self.share(-step)

    def e3(self):
        for step in (1, -1):
            self.messages.got((self.name, "yh", step))
        self.share(2)

    def e6(self):
        for dy in (0, 1, -1, 2):
            self.messages.got((self.name, "s", dy))


MESSAGES = 4 * 20 + 2 * 8


def gather_kernel(
    row_ranks, column_ranks, trailing, row_left, row_right, column_left, column_right,
    out,
    col_v, col_u, row_v, row_u, total, core, right, dense, send_sem, recv_sem, local_sem,
):
    grid = Grid()
    panels, tiles, depth_r, width = row_left.shape
    depth_c = column_left.shape[2]
    chunk = SIDE * depth_c
    loads = []
    for tile in range(2):
        for source, target in ((column_right, col_v), (column_left, col_u)):
            loads.append((source.at[:, tile], target.at[tile, :, grid.z, grid.x]))
        lanes = pl.ds(tile * width, width)
        loads.append((row_right.at[:, tile], row_v.at[:, grid.y, grid.core, :, lanes]))
    for panel in range(panels):
        lanes = pl.ds(panel * width, width)
        loads.append((row_left.at[panel], row_u.at[:, grid.y, grid.core, :, lanes]))
    loads.append((trailing, dense))
    loads = [
        pltpu.make_async_copy(source, target, local_sem.at[n])
        for n, (source, target) in enumerate(loads)
    ]
    for load in loads:
        load.start()
    barrier = pltpu.get_barrier_semaphore()
    for axis, step in (("x", 1), ("x", -1), ("z", 1), ("z", -1), ("y", 1), ("y", -1), ("core", 1)):
        pl.semaphore_signal(
            barrier, inc=1, device_id=grid.neighbour(axis, step), device_id_type=MESH
        )
    pl.semaphore_wait(barrier, 7)
    for load in loads[:-1]:
        load.wait()

    messages = Messages(send_sem, recv_sem)
    v = [
        ColumnStream("v0", grid, messages, col_v.at[0], "x", "z"),
        ColumnStream("v1", grid, messages, col_v.at[1], "z", "x"),
    ]
    u = [
        ColumnStream("u0", grid, messages, col_u.at[0], "x", "z"),
        ColumnStream("u1", grid, messages, col_u.at[1], "z", "x"),
    ]
    rv = [RowStream("rv", grid, messages, row_v)]
    ru = [RowStream("ru", grid, messages, row_u)]

    def all_of(streams, *names):
        for name in names:
            for stream in streams:
                getattr(stream, name)()

    def widen():
        def one(turn, carry):
            rows = pl.ds(pl.multiple_of((turn % 4) * chunk, chunk), chunk)
            out[turn // 4, 1, rows] = dense[turn // 4, 1, rows].astype(jnp.float32)
            return carry

        lax.fori_loop(0, 4 * tiles, one, 0)

    def cores(col, step, first=False, last=False):
        place = grid.shifted("z" if col == 0 else "x", step)

        def one(panel, carry):
            if col == 0:
                left_side, right_side = col_v[0, panel, place], row_v[panel, place]
            else:
                start = pl.multiple_of((place % 2) * depth_c, depth_c)
                left_side = col_v[1, panel, :, place]
                right_side = row_v[panel, :, place // 2, pl.ds(start, depth_c)]
            value = lax.dot_general(
                left_side.reshape(chunk, width),
                right_side.reshape(chunk, tiles * width),
                (((0,), (0,)), ((), ())),
                preferred_element_type=jnp.float32,
            )
            if not first:
                value = value + total[col, panel]
            if last:
                shape = value.shape
                lane = lax.broadcasted_iota(jnp.int32, shape, 1)
                limit = jnp.where(
                    lane < width,
                    row_ranks[panel, grid.r * 2],
                    row_ranks[panel, grid.r * 2 + 1] + width,
                )
                keep = (lane < limit) & (
                    lax.broadcasted_iota(jnp.int32, shape, 0) < column_ranks[col, panel]
                )
                core[col, panel] = jnp.where(keep, value, 0.0).astype(core.dtype)
            else:
                total[col, panel] = value
            return carry

        lax.fori_loop(0, panels, one, 0)

    def updates(col, step):
        place = grid.shifted("z" if col == 0 else "x", step)
        half = place % 2
        for panel in range(panels):
            factor = col_u[0, panel, place] if col == 0 else col_u[1, panel, :, place]
            value = jnp.dot(
                factor.reshape(chunk, width), core[col, panel], preferred_element_type=jnp.float32
            ).astype(right.dtype)
            for tile in range(tiles):
                lanes = pl.ds(panel * width, width)
                piece = value[:, tile * width : (tile + 1) * width]
                if col == 0:
                    right[tile, :, lanes] = piece
                    continue
                for group in range(SIDE):
                    side = half if group < 2 else 1 - half
                    start = pl.multiple_of((group % 2) * 2 * depth_c + side * depth_c, depth_c)
                    right[tile, pl.ds(start, depth_c), lanes] = piece[
                        group * depth_c : (group + 1) * depth_c
                    ]

        def one(turn, carry):
            tile, part = turn // 2, turn % 2
            rows = 2 * chunk
            value = lax.dot_general(
                row_u[tile, pl.ds(part * 2, 2)].reshape(rows, panels * width),
                right[tile],
                (((1,), (1,)), ((), ())),
                preferred_element_type=jnp.float32,
            )
            here = pl.ds(pl.multiple_of(part * rows, rows), rows)
            if col == 0:
                lanes = pl.ds(pl.multiple_of(place * chunk, chunk), chunk)
                out[tile, 0, here, lanes] = dense[tile, 0, here, lanes].astype(jnp.float32) - value
                return carry
            span = 2 * depth_c
            mine = lax.broadcasted_iota(jnp.int32, (rows, span), 1) // depth_c == half
            for group in range(SIDE):
                piece = value[:, (group % 2) * span : (group % 2 + 1) * span]
                if group >= 2:
                    piece = pltpu.roll(piece, depth_c, 1)
                lanes = pl.ds(pl.multiple_of((group * 2 + place // 2) * span, span), span)
                out[tile, 1, here, lanes] = out[tile, 1, here, lanes] - jnp.where(mine, piece, 0.0)
            return carry

        lax.fori_loop(0, 2 * tiles, one, 0)

    all_of(v, "start_a", "start_b")
    all_of(rv, "start")
    all_of(v, "e1")
    loads[-1].wait()
    widen()
    all_of(v, "e2")
    all_of(rv, "e1")
    all_of(v, "e3")
    all_of(u, "start_a", "start_b")
    all_of(rv, "e3")
    all_of(ru, "start")
    all_of(v, "e4", "e5")
    all_of(u, "e1")
    all_of(rv, "e6")
    for col in range(2):
        cores(col, 0, first=True)
    all_of(u, "e2")
    for col in range(2):
        cores(col, 1)
    all_of(ru, "e1")
    for col in range(2):
        cores(col, -1)
    all_of(u, "e3")
    all_of(v, "e6")
    for col in range(2):
        cores(col, 2, last=True)
    all_of(u, "e4")
    all_of(ru, "e3", "e6")
    updates(0, 0)
    updates(1, 0)
    all_of(u, "e5")
    for step in (1, -1):
        for col in range(2):
            updates(col, step)
    for col in range(2):
        u[col].e6()
        updates(col, 2)
    messages.drain()


def on_device(trailing, row_left, row_right, column_left, column_right, row_ranks, column_ranks):
    panels, tiles, depth_r, width = row_left.shape
    depth_c = column_left.shape[2]
    order = trailing.shape[3]
    bf16 = jnp.bfloat16
    any_space = pl.BlockSpec(memory_space=pl.ANY)
    smem = pl.BlockSpec(memory_space=pltpu.SMEM)
    col_shape = (2, panels, SIDE, SIDE, depth_c, width)
    return pl.pallas_call(
        gather_kernel,
        out_shape=pltpu.VMEM(trailing.shape, jnp.float32),
        in_specs=[smem, smem] + [any_space] * 5,
        out_specs=pl.BlockSpec(memory_space=pltpu.VMEM),
        scratch_shapes=[
            pltpu.VMEM(col_shape, bf16),
            pltpu.VMEM(col_shape, bf16),
            pltpu.VMEM((panels, SIDE, 2, depth_r, tiles * width), bf16),
            pltpu.VMEM((tiles, SIDE, 2, depth_r, panels * width), bf16),
            pltpu.VMEM((2, panels, width, tiles * width), jnp.float32),
            pltpu.VMEM((2, panels, width, tiles * width), bf16),
            pltpu.VMEM((tiles, SIDE * depth_c, panels * width), bf16),
            pltpu.VMEM(trailing.shape, bf16),
            pltpu.SemaphoreType.DMA((MESSAGES,)),
            pltpu.SemaphoreType.DMA((MESSAGES,)),
            pltpu.SemaphoreType.DMA((10,)),
        ],
        compiler_params=pltpu.CompilerParams(
            collective_id=0, has_side_effects=True, vmem_limit_bytes=LIMIT
        ),
        name="gather_update",
    )(row_ranks, column_ranks.T, trailing, row_left, row_right, column_left, column_right)


LIMIT = 46 << 20


def solution(mesh):
    return jax.shard_map(
        on_device,
        mesh=mesh,
        in_specs=(
            P("rows", "cols", None, None),
            P(None, "rows", "cols", None),
            P(None, "rows", "cols", None),
            P(None, "cols", "rows", None),
            P(None, "cols", "rows", None),
            P(),
            P(None, "cols"),
        ),
        out_specs=P("rows", "cols", None, None),
        check_vma=False,
    )
```
